512 devices in a mesh: doc: 16 (over z, core), gram: 32 (over x, y).
Axes of the slice: x: 4, y: 8, z: 8, core: 2. Of those that a mesh axis runs over, the one named last changes fastest.
Arguments:
- w_factor: bfloat16 [24576, 256], P(('doc', 'gram')), may hold values from 0.003 to 0.1
- h_factor: bfloat16 [49152, 256], P(('gram', 'doc')), may hold values from 0.003 to 0.1
- tile_counts: bfloat16 [16, 32, 24, 128, 128], P('doc', 'gram'), may hold values from 0 to 30, as said below
- tile_rows: int32 [16, 32, 24], P('doc', 'gram'), may hold values from 0 to 11, as said below
- tile_cols: int32 [16, 32, 24], P('doc', 'gram'), may hold values from 0 to 11, as said below
- tile_live: int32 [16, 32], P('doc', 'gram'), may hold values from 1 to 24, as said below
Outputs:
- w_next: bfloat16 [24576, 256], P(('doc', 'gram'))
- h_next: bfloat16 [49152, 256], P(('gram', 'doc'))
The draws below stay inside these ranges and needn't reach their ends.
Inputs may be any that keep to these rules, and one draw needn't show every extreme that they name: `tile_rows`: within one device pair the first tile_live slots name distinct tiles; slots hold positions in every case. `tile_cols`: see tile_rows. `tile_live`: some device pair holds 24 tiles. `tile_counts`: whole numbers.
All inputs are finite; a program needn't handle non-finite values.
Results may differ from the reference program's by a relative error of at most 0.0021.
Values may be sent and summed in bfloat16 or wider, within the bound.
A program may use at most 64 MiB of HBM per device.

```python
import jax
import jax.numpy as jnp
from jax import lax

TOPICS = 256
TILE = 128
TR = 12
TC = 12
SLOTS = 24
DOCS = 24576
NGRAMS = 49152
N_DOC = 16
N_GRAM = 32


def draw_w_factor(key, part):
    place = jnp.arange(DOCS, dtype=jnp.float32)[:, None]
    rising = 1.0 + 2.0 * place / DOCS
    base = 0.01 * jnp.exp(jax.random.uniform(key, (DOCS, TOPICS), jnp.float32, -1.0, 1.0))
    return (base * rising).astype(jnp.bfloat16)


def draw_h_factor(key, part):
    place = jnp.arange(NGRAMS, dtype=jnp.float32)[:, None]
    rising = 1.0 + 2.0 * place / NGRAMS
    base = 0.01 * jnp.exp(jax.random.uniform(key, (NGRAMS, TOPICS), jnp.float32, -1.0, 1.0))
    return (base * rising).astype(jnp.bfloat16)


def draw_tile_counts(key, part):
    shape = (N_DOC, N_GRAM, SLOTS, TILE, TILE)
    first, second = jax.random.split(key)
    present = jax.random.randint(first, shape, 0, 5) < 2
    values = jax.random.randint(second, shape, 1, 16)
    return jnp.where(present, values, 0).astype(jnp.float32).astype(jnp.bfloat16)


def tile_places(key):
    base = jax.random.fold_in(key, 7)
    keys = jax.random.split(base, N_DOC * N_GRAM)
    orders = jax.vmap(lambda one: jax.random.permutation(one, TR * TC))(keys)[:, :SLOTS]
    return orders.reshape(N_DOC, N_GRAM, SLOTS).astype(jnp.int32)


def draw_tile_rows(key, part):
    return tile_places(key) // TC


def draw_tile_cols(key, part):
    return tile_places(key) % TC


def draw_tile_live(key, part):
    base = jax.random.fold_in(key, 11)
    lots = jax.random.randint(base, (N_DOC * N_GRAM,), SLOTS // 4, SLOTS + 1)
    chosen = jax.random.randint(jax.random.fold_in(base, 3), (), 0, N_DOC * N_GRAM)
    lots = jnp.where(jnp.arange(N_DOC * N_GRAM, dtype=jnp.int32) == chosen, SLOTS, lots)
    return lots.reshape(N_DOC, N_GRAM).astype(jnp.int32)


def setup_inputs(seed: int = 0) -> dict:
    streams_of = jax.random.split(jax.random.key(seed), 7)
    return {
        "w_factor": draw_w_factor(jax.random.fold_in(streams_of[6], 71), 0),
        "h_factor": draw_h_factor(jax.random.fold_in(streams_of[6], 71), 0),
        "tile_counts": draw_tile_counts(jax.random.fold_in(streams_of[6], 71), 0),
        "tile_rows": draw_tile_rows(jax.random.fold_in(streams_of[6], 71), 0),
        "tile_cols": draw_tile_cols(jax.random.fold_in(streams_of[6], 71), 0),
        "tile_live": draw_tile_live(jax.random.fold_in(streams_of[6], 71), 0),
    }


def pair_terms(w_tiles, h_tiles, rows, cols, counts, live):
    width = rows.shape[0]
    wt = jnp.take(w_tiles, rows, axis=0).astype(jnp.float32)
    ht = jnp.take(h_tiles, cols, axis=0).astype(jnp.float32)
    model = jnp.einsum('spk,sqk->spq', wt, ht)
    keep = (jnp.arange(width, dtype=jnp.int32) < live).astype(jnp.float32)
    ratio = (counts.astype(jnp.float32) / model * keep[:, None, None]).astype(jnp.bfloat16)
    ratio_f = ratio.astype(jnp.float32)
    w_part = jnp.einsum('spq,sqk->spk', ratio_f, ht)
    h_part = jnp.einsum('spq,spk->sqk', ratio_f, wt)
    pick_r = (rows[:, None] == jnp.arange(w_tiles.shape[0], dtype=jnp.int32)[None, :]).astype(jnp.float32)
    pick_c = (cols[:, None] == jnp.arange(h_tiles.shape[0], dtype=jnp.int32)[None, :]).astype(jnp.float32)
    add_w = jnp.einsum('st,spk->tpk', pick_r, w_part, precision=lax.Precision.HIGHEST)
    add_h = jnp.einsum('st,spk->tpk', pick_c, h_part, precision=lax.Precision.HIGHEST)
    return add_w, add_h


def reference(w_factor, h_factor, tile_counts, tile_rows, tile_cols, tile_live):
    w_blocks = w_factor.reshape(N_DOC, TR, TILE, TOPICS)
    h_blocks = h_factor.reshape(N_GRAM, TC, TILE, TOPICS)
    pairs = jnp.arange(N_DOC * N_GRAM, dtype=jnp.int32)

    def visit(carry, pair):
        w_numer, h_numer = carry
        d = pair // N_GRAM
        g = pair % N_GRAM
        add_w, add_h = pair_terms(w_blocks[d], h_blocks[g], tile_rows[d, g], tile_cols[d, g], tile_counts[d, g], tile_live[d, g])
        return (w_numer.at[d].add(add_w), h_numer.at[g].add(add_h)), None

    start = (jnp.zeros((N_DOC, TR, TILE, TOPICS), jnp.float32), jnp.zeros((N_GRAM, TC, TILE, TOPICS), jnp.float32))
    (w_numer, h_numer), _ = lax.scan(visit, start, pairs)
    w_denom = jnp.sum(h_factor.astype(jnp.float32), axis=0)
    h_denom = jnp.sum(w_factor.astype(jnp.float32), axis=0)
    w_next = (w_factor.astype(jnp.float32) * w_numer.reshape(DOCS, TOPICS) / w_denom).astype(jnp.bfloat16)
    h_next = (h_factor.astype(jnp.float32) * h_numer.reshape(NGRAMS, TOPICS) / h_denom).astype(jnp.bfloat16)
    return w_next, h_next
```

```python
import functools

import jax
import jax.numpy as jnp
from jax import lax
from jax.experimental import pallas as pl
from jax.experimental.pallas import tpu as pltpu
from jax.sharding import PartitionSpec as P

MESH = pl.DeviceIdType.MESH
NC = 2
SUB = 16
F32 = jnp.float32
BF16 = jnp.bfloat16


def encode(v):
    s = v * v
    return (s * s).astype(BF16)


def decode(code):
    return lax.rsqrt(lax.rsqrt(code.astype(F32)))


def kernel(nx, ny, nz, tr, tc, slots, tile,
           rows_s, cols_s, map_s, w_ref, h_ref, counts_hbm, wo_ref, ho_ref,
           wbuf, hbuf, counts, rat, rat_t, wfull, wp, hfull, hp,
           wa_in, wa_mid, wa_in2, wb_in, wb_mid, wb_in2, hc_in, hz_mid, hz_in,
           cs_out, cs_x_in, cs_mid, cs_y_in, cd_out, cd_c_in, cd_mid, cd_z_in,
           loc_sem, ss, rs):
    doc = lax.axis_index("doc")
    gram = lax.axis_index("gram")
    z, c = doc // NC, lax.rem(doc, NC)
    x, y = gram // ny, lax.rem(gram, ny)
    jw = wbuf.shape[1] // ny
    ja = jw - 1
    jh = hbuf.shape[0] // (nz * NC)
    gpt = tile // SUB
    topics = w_ref.shape[-1]

    count = [0]

    def rcopy(src, dst, to_doc, to_gram):
        i = count[0]
        count[0] += 1
        return pltpu.make_async_remote_copy(
            src_ref=src, dst_ref=dst, send_sem=ss.at[i], recv_sem=rs.at[i],
            device_id=(to_doc, to_gram), device_id_type=MESH)

    def at_x(k):
        return lax.rem(x + k, nx)

    def at_y(k):
        return lax.rem(y + k, ny)

    def at_z(k):
        return lax.rem(z + k, nz)

    def far_first(n):
        return sorted(range(1, n), key=lambda k: -min(k, n - k))

    partner = z * NC + (1 - c)

    counts_copy = pltpu.make_async_copy(counts_hbm, counts, loc_sem)
    counts_copy.start()
    wbuf[x, pl.ds(y * jw, jw)] = w_ref[...]
    hbuf[pl.ds(doc * jh, jh)] = h_ref[...]

    barrier = pltpu.get_barrier_semaphore()
    peers = 0
    for k in range(1, nx):
        pl.semaphore_signal(barrier, inc=1, device_id=(doc, at_x(k) * ny + y), device_id_type=MESH)
        peers += 1
    for k in range(1, ny):
        pl.semaphore_signal(barrier, inc=1, device_id=(doc, x * ny + at_y(k)), device_id_type=MESH)
        peers += 1
    for k in range(1, nz):
        pl.semaphore_signal(barrier, inc=1, device_id=(at_z(k) * NC + c, gram), device_id_type=MESH)
        peers += 1
    pl.semaphore_signal(barrier, inc=1, device_id=(partner, gram), device_id_type=MESH)
    peers += 1
    rat[slots] = jnp.zeros((tile, tile), BF16)
    rat_t[slots] = jnp.zeros((tile, tile), BF16)
    pl.semaphore_wait(barrier, peers)

    ag_hz = []
    for k in far_first(nz):
        cp = rcopy(h_ref, hbuf.at[pl.ds(doc * jh, jh)], at_z(k) * NC + c, gram)
        cp.start()
        ag_hz.append((k, cp))
    ag_ay = []
    for k in far_first(ny):
        cp = rcopy(w_ref.at[pl.ds(0, ja)], wbuf.at[x, pl.ds(y * jw, ja)], doc, x * ny + at_y(k))
        cp.start()
        ag_ay.append(cp)
    ag_bx = []
    for k in far_first(nx):
        cp = rcopy(w_ref.at[pl.ds(ja, 1)], wbuf.at[x, pl.ds(y * jw + ja, 1)], doc, at_x(k) * ny + y)
        cp.start()
        ag_bx.append(cp)
    ag_hc = [rcopy(h_ref, hbuf.at[pl.ds(doc * jh, jh)], partner, gram)]
    ag_hc[0].start()
    for cp in ag_bx:
        cp.wait_recv()
    ag_by = []
    for k in far_first(ny):
        piece = wbuf.at[:, pl.ds(y * jw + ja, 1)]
        cp = rcopy(piece, piece, doc, x * ny + at_y(k))
        cp.start()
        ag_by.append(cp)
    for cp in ag_ay:
        cp.wait_recv()
    ag_ax = []
    for k in far_first(nx):
        per_y = []
        for yy in range(ny):
            piece = wbuf.at[x, pl.ds(yy * jw, ja)]
            cp = rcopy(piece, piece, doc, at_x(k) * ny + y)
            cp.start()
            per_y.append(cp)
        ag_ax.append(per_y)
    for k, cp in reversed(ag_hz):
        cp.wait_recv()
        came = lax.rem(z + nz - k, nz) * NC + c
        piece = hbuf.at[pl.ds(came * jh, jh)]
        fw = rcopy(piece, piece, partner, gram)
        fw.start()
        ag_hc.append(fw)
    for cp in ag_hc:
        cp.wait_recv()
    for per_y in ag_ax:
        for cp in per_y:
            cp.wait_recv()
    for cp in ag_by:
        cp.wait_recv()

    ones = jnp.ones((8, tile), BF16)

    def w_tile(r):
        per = (ny * jw) // gpt
        return wbuf[r // per, pl.ds(lax.rem(r, per) * gpt, gpt)].reshape(tile, topics)

    def h_tile(q):
        return hbuf[pl.ds(q * gpt, gpt)].reshape(tile, topics)

    sum_h = jnp.zeros((8, topics), F32)
    for q in range(tc):
        sum_h += jnp.dot(ones, h_tile(q), preferred_element_type=F32)
    cs_out[...] = sum_h
    sum_w = jnp.zeros((8, topics), F32)
    for r in range(tr):
        sum_w += jnp.dot(ones, w_tile(r), preferred_element_type=F32)
    cd_out[...] = sum_w

    counts_copy.wait()

    def ratio_step(i, carry):
        for u in range(4):
            s = i * 4 + u
            wt = w_tile(rows_s[s])
            ht = h_tile(cols_s[s])
            model = lax.dot_general(wt, ht, (((1,), (1,)), ((), ())), preferred_element_type=F32)
            ratio = counts[s].astype(F32) / model
            rat[s] = ratio.astype(BF16)
            rat_t[s] = ratio.T.astype(BF16)
        return carry

    lax.fori_loop(0, slots // 4, ratio_step, 0)

    cs_x = []
    for k in range(1, nx):
        cp = rcopy(cs_out, cs_x_in.at[k - 1], doc, at_x(k) * ny + y)
        cp.start()
        cs_x.append(cp)
    cd_c = rcopy(cd_out, cd_c_in, partner, gram)
    cd_c.start()

    wg = tr // nx
    zg = max(1, nz // 4)
    hg = tc * zg // nz
    h_all = hbuf[...].reshape(tc * tile, topics)
    rs_ax = []
    for k in range(1, nx + 1):
        xx = at_x(k)
        lhs = jnp.concatenate([
            jnp.concatenate([rat[map_s[(xx * wg + i) * tc + q]] for q in range(tc)], axis=1)
            for i in range(wg)], axis=0)
        out = jnp.dot(lhs, hbuf[...].reshape(tc * tile, topics), preferred_element_type=F32)
        out = out.reshape(ny * jw, SUB, topics)
        wfull[xx] = out
        wp[xx] = encode(out)
        if k < nx:
            per_y = []
            for yy in range(ny):
                cp = rcopy(wp.at[xx, pl.ds(yy * jw, ja)], wa_in.at[k - 1, pl.ds(yy * ja, ja)],
                           doc, xx * ny + y)
                cp.start()
                per_y.append(cp)
            rs_ax.append(per_y)
    rs_by = []
    for k in far_first(ny):
        yy = at_y(k)
        cp = rcopy(wp.at[:, pl.ds(yy * jw + ja, 1)], wb_in.at[k - 1], doc, x * ny + yy)
        cp.start()
        rs_by.append(cp)
    rs_hc = []
    for k in range(1, nz // zg + 1):
        qq = lax.rem(z // zg + k, nz // zg)
        lhs = jnp.concatenate([
            jnp.concatenate([rat_t[map_s[r * tc + qq * hg + i]] for r in range(tr)], axis=1)
            for i in range(hg)], axis=0)
        out = jnp.dot(lhs, wbuf[...].reshape(tr * tile, topics), preferred_element_type=F32)
        out = out.reshape(hg * gpt, SUB, topics)
        hfull[pl.ds(qq * hg * gpt, hg * gpt)] = out
        hp[pl.ds(qq * hg * gpt, hg * gpt)] = encode(out)
        for i in range(zg):
            zz = qq * zg + i
            cp = rcopy(hp.at[pl.ds((zz * NC + 1 - c) * jh, jh)], hc_in.at[zz], partner, gram)
            cp.start()
            rs_hc.append((zz, cp))

    for per_y in rs_ax:
        for cp in per_y:
            cp.wait_recv()
    rs_ay = []
    for yy in range(ny):
        total = wfull[x, pl.ds(yy * jw, ja)]
        for k in range(nx - 1):
            total += decode(wa_in[k, pl.ds(yy * ja, ja)])
        wfull[x, pl.ds(yy * jw, ja)] = total
        wa_mid[yy] = encode(total)
    for k in far_first(ny):
        yy = at_y(k)
        cp = rcopy(wa_mid.at[yy], wa_in2.at[k - 1], doc, x * ny + yy)
        cp.start()
        rs_ay.append(cp)
    rs_hz = []
    for zz, cp in rs_hc:
        cp.wait_recv()
    for k in far_first(nz):
        zz = at_z(k)
        total = hfull[pl.ds((zz * NC + c) * jh, jh)] + decode(hc_in[zz])
        hz_mid[k - 1] = encode(total)
        cp = rcopy(hz_mid.at[k - 1], hz_in.at[k - 1], zz * NC + c, gram)
        cp.start()
        rs_hz.append((k, cp))
    for cp in rs_by:
        cp.wait_recv()
    total_b = wfull[:, pl.ds(y * jw + ja, 1)]
    for k in range(ny - 1):
        total_b += decode(wb_in[k])
    wfull[:, pl.ds(y * jw + ja, 1)] = total_b
    wb_mid[...] = encode(total_b)
    rs_bx = []
    for k in far_first(nx):
        xx = at_x(k)
        cp = rcopy(wb_mid.at[xx], wb_in2.at[k - 1], doc, xx * ny + y)
        cp.start()
        rs_bx.append(cp)
    for cp in cs_x:
        cp.wait_recv()
    part = cs_out[...]
    for k in range(nx - 1):
        part += cs_x_in[k]
    cs_mid[...] = part
    cs_y = []
    for k in range(1, ny):
        cp = rcopy(cs_mid, cs_y_in.at[k - 1], doc, x * ny + at_y(k))
        cp.start()
        cs_y.append(cp)
    cd_c.wait_recv()
    cd_mid[...] = cd_out[...] + cd_c_in[...]
    cd_z = []
    for k in range(1, nz):
        cp = rcopy(cd_mid, cd_z_in.at[k - 1], at_z(k) * NC + c, gram)
        cp.start()
        cd_z.append(cp)

    own_h = hfull[pl.ds(doc * jh, jh)] + decode(hc_in[z])
    for k, cp in rs_hz:
        cp.wait_recv()
    for k in range(nz - 1):
        own_h += decode(hz_in[k])
    for cp in cd_z:
        cp.wait_recv()
    h_den = cd_mid[...]
    for k in range(nz - 1):
        h_den += cd_z_in[k]
    ho_ref[...] = (h_ref[...].astype(F32) * own_h / h_den[0:1].reshape(1, 1, topics)).astype(BF16)

    for cp in cs_y:
        cp.wait_recv()
    w_den = cs_mid[...]
    for k in range(ny - 1):
        w_den += cs_y_in[k]
    w_den = w_den[0:1].reshape(1, 1, topics)
    for cp in rs_ay:
        cp.wait_recv()
    own_a = wfull[x, pl.ds(y * jw, ja)]
    for k in range(ny - 1):
        own_a += decode(wa_in2[k])
    wo_ref[pl.ds(0, ja)] = (w_ref[pl.ds(0, ja)].astype(F32) * own_a / w_den).astype(BF16)
    for cp in rs_bx:
        cp.wait_recv()
    own_b = wfull[x, pl.ds(y * jw + ja, 1)]
    for k in range(nx - 1):
        own_b += decode(wb_in2[k])
    wo_ref[pl.ds(ja, 1)] = (w_ref[pl.ds(ja, 1)].astype(F32) * own_b / w_den).astype(BF16)

    sends = [cp for _, cp in ag_hz] + ag_ay + ag_bx + ag_hc + ag_by + sum(ag_ax, [])
    sends += cs_x + [cd_c] + sum(rs_ax, []) + rs_by + [cp for _, cp in rs_hc] + rs_ay
    sends += [cp for _, cp in rs_hz] + rs_bx + cs_y + cd_z
    for cp in sends:
        cp.wait_send()


def copies(nx, ny, nz):
    gather = (nz - 1) + (ny - 1) + (nx - 1) + nz + (ny - 1) + (nx - 1) * ny
    scatter = (nx - 1) * ny + (ny - 1) + nz + (ny - 1) + (nz - 1) + (nx - 1)
    sums = (nx - 1) + 1 + (ny - 1) + (nz - 1)
    return gather + scatter + sums


def body(nx, ny, nz, w_factor, h_factor, tile_counts, tile_rows, tile_cols, tile_live):
    topics = w_factor.shape[1]
    slots, tile = tile_counts.shape[2], tile_counts.shape[3]
    tr = w_factor.shape[0] * nx * ny // tile
    tc = h_factor.shape[0] * nz * NC // tile
    rows, cols, live = tile_rows[0, 0], tile_cols[0, 0], tile_live[0, 0]
    jw, jh = w_factor.shape[0] // SUB, h_factor.shape[0] // SUB
    ja = jw - 1
    order = jnp.arange(slots, dtype=jnp.int32)
    hit = (rows * tc + cols)[None, :] == jnp.arange(tr * tc, dtype=jnp.int32)[:, None]
    hit = hit & (order < live)[None, :]
    place = jnp.min(jnp.where(hit, order[None, :], slots), axis=1)

    vmem = pl.BlockSpec(memory_space=pltpu.VMEM)
    smem = pl.BlockSpec(memory_space=pltpu.SMEM)
    n = copies(nx, ny, nz)
    V = pltpu.VMEM
    w_next, h_next = pl.pallas_call(
        functools.partial(kernel, nx, ny, nz, tr, tc, slots, tile),
        out_shape=(jax.ShapeDtypeStruct((jw, SUB, topics), BF16),
                   jax.ShapeDtypeStruct((jh, SUB, topics), BF16)),
        in_specs=[smem, smem, smem, vmem, vmem, pl.BlockSpec(memory_space=pl.ANY)],
        out_specs=(vmem, vmem),
        scratch_shapes=[
            V((nx, ny * jw, SUB, topics), BF16),
            V((nz * NC * jh, SUB, topics), BF16),
            V((slots, tile, tile), BF16),
            V((slots + 1, tile, tile), BF16),
            V((slots + 1, tile, tile), BF16),
            V((nx, ny * jw, SUB, topics), F32),
            V((nx, ny * jw, SUB, topics), BF16),
            V((nz * NC * jh, SUB, topics), F32),
            V((nz * NC * jh, SUB, topics), BF16),
            V((nx - 1, ny * ja, SUB, topics), BF16),
            V((ny, ja, SUB, topics), BF16),
            V((ny - 1, ja, SUB, topics), BF16),
            V((ny - 1, nx, 1, SUB, topics), BF16),
            V((nx, 1, SUB, topics), BF16),
            V((nx - 1, 1, SUB, topics), BF16),
            V((nz, jh, SUB, topics), BF16),
            V((nz - 1, jh, SUB, topics), BF16),
            V((nz - 1, jh, SUB, topics), BF16),
            V((8, topics), F32),
            V((nx - 1, 8, topics), F32),
            V((8, topics), F32),
            V((ny - 1, 8, topics), F32),
            V((8, topics), F32),
            V((8, topics), F32),
            V((8, topics), F32),
            V((nz - 1, 8, topics), F32),
            pltpu.SemaphoreType.DMA(()),
            pltpu.SemaphoreType.DMA((n,)),
            pltpu.SemaphoreType.DMA((n,)),
        ],
        compiler_params=pltpu.CompilerParams(
            collective_id=0, has_side_effects=True, vmem_limit_bytes=56 << 20),
        name="update",
    )(rows, cols, place, w_factor.reshape(jw, SUB, topics), h_factor.reshape(jh, SUB, topics),
      tile_counts.reshape(slots, tile, tile))
    return w_next.reshape(w_factor.shape), h_next.reshape(h_factor.shape)


def solution(mesh, nx=4, nz=8):
    ny = mesh.shape["gram"] // nx
    in_specs = (
        P(("doc", "gram"), None),
        P(("gram", "doc"), None),
        P("doc", "gram", None, None, None),
        P("doc", "gram", None),
        P("doc", "gram", None),
        P("doc", "gram"),
    )
    out_specs = (P(("doc", "gram"), None), P(("gram", "doc"), None))
    return jax.shard_map(functools.partial(body, nx, ny, nz), mesh=mesh, in_specs=in_specs,
                         out_specs=out_specs, check_vma=False)
```

```python
import functools

import jax
import jax.numpy as jnp
from jax import lax
from jax.experimental import pallas as pl
from jax.experimental.pallas import tpu as pltpu
from jax.sharding import PartitionSpec as P

MESH = pl.DeviceIdType.MESH
NX, NY, NZ, NC = 4, 8, 8, 2
SUB = 16
F32 = jnp.float32
BF16 = jnp.bfloat16
NEAR = (1, 7, 2, 6, 3, 5, 4)
FAR = (4, 3, 5, 2, 6, 1, 7)


def encode(v):
    s = v * v
    return (s * s).astype(BF16)


def decode(code):
    return lax.rsqrt(lax.rsqrt(code.astype(F32)))


def kernel(tr, tc, slots, tile,
           rows_s, cols_s, live_s, w_ref, h_ref, counts_hbm, wo_ref, ho_ref,
           wbuf, hbuf, counts, rat, rat_t, wfull, wp, hfull, hp,
           wx_in, wy_mid, wy_in, hc_in, hz_mid, h3_in, h4_in, hz_in,
           cs_out, cs_x_in, cs_mid, cs_y_in, cd_out, cd_c_in, cd_mid, cd_z_in,
           map_v, map_s, loc_sem, map_sem, ss, rs):
    doc = lax.axis_index("doc")
    gram = lax.axis_index("gram")
    z, c = doc // NC, lax.rem(doc, NC)
    x, y = gram // NY, lax.rem(gram, NY)
    jw = wbuf.shape[1] // NY
    jh = hbuf.shape[0] // (NZ * NC)
    hh = jh // 2
    gpt = tile // SUB
    topics = w_ref.shape[-1]
    sent = []

    def send(src, dst, to):
        i = len(sent)
        cp = pltpu.make_async_remote_copy(
            src_ref=src, dst_ref=dst, send_sem=ss.at[i], recv_sem=rs.at[i],
            device_id=to, device_id_type=MESH)
        cp.start()
        sent.append(cp)
        return cp

    def at_x(k):
        return lax.rem(x + NX + k, NX)

    def at_y(k):
        return lax.rem(y + NY + k, NY)

    def at_z(k):
        return lax.rem(z + NZ + k, NZ)

    def to_x(k):
        return doc, at_x(k) * NY + y

    def to_y(k):
        return doc, x * NY + at_y(k)

    def to_z(k):
        return at_z(k) * NC + c, gram

    partner = (z * NC + (1 - c), gram)

    barrier = pltpu.get_barrier_semaphore()
    peers = [to_y(k) for k in FAR] + [to_z(k) for k in FAR] + [to_x(k) for k in (2, 1, 3)] + [partner]
    for peer in peers:
        pl.semaphore_signal(barrier, inc=1, device_id=peer, device_id_type=MESH)
    counts_copy = pltpu.make_async_copy(counts_hbm, counts, loc_sem)
    counts_copy.start()
    wbuf[x, pl.ds(y * jw, jw)] = w_ref[...]
    hbuf[pl.ds(doc * jh, jh)] = h_ref[...]
    pl.semaphore_wait(barrier, len(peers))

    def w_piece(k):
        return wbuf.at[x, pl.ds(at_y(k) * jw, jw)]

    def h_piece(k):
        return hbuf.at[pl.ds((at_z(k) * NC + c) * jh, jh)]

    def h_half(k, i):
        return hbuf.at[pl.ds((at_z(k) * NC + c) * jh + i * hh, hh)]

    gx = [send(w_ref, w_piece(0), to_x(k)) for k in (1, 3, 2)]
    gy = {k: send(w_ref, w_piece(0), to_y(k)) for k in NEAR}
    p2 = send(h_ref, h_piece(0), to_z(2))
    m2 = send(h_ref, h_piece(0), to_z(-2))
    p1 = send(h_ref, h_piece(0), to_z(1))
    m1 = send(h_ref, h_piece(0), to_z(-1))
    gc = [send(h_ref, h_piece(0), partner)]

    at_row = lax.broadcasted_iota(jnp.int32, map_v.shape, 0)
    at_col = lax.broadcasted_iota(jnp.int32, map_v.shape, 1)
    place = jnp.full(map_v.shape, slots, jnp.int32)
    for s in range(slots):
        row = jnp.where(s < live_s[0, 0], rows_s[s], -1)
        place = jnp.where((at_row == row) & (at_col == cols_s[s]), s, place)
    map_v[...] = place
    rat[slots] = jnp.zeros((tile, tile), BF16)
    rat_t[slots] = jnp.zeros((tile, tile), BF16)

    def w_on(ks):
        for k in ks:
            gy[k].wait_recv()
            gx.extend(send(w_piece(-k), w_piece(-k), to_x(j)) for j in (1, 3, 2))

    w_on((1, 7, 2, 6))
    map_copy = pltpu.make_async_copy(map_v, map_s, map_sem)
    map_copy.start()
    p2.wait_recv()
    p3 = send(h_piece(-2), h_piece(-2), to_z(1))
    p4 = send(h_half(-2, 0), h_half(-2, 0), to_z(2))
    m2.wait_recv()
    m3 = send(h_piece(2), h_piece(2), to_z(-1))
    m4 = send(h_half(2, 1), h_half(2, 1), to_z(-2))
    gc += [send(h_piece(-2), h_piece(-2), partner), send(h_piece(2), h_piece(2), partner)]
    w_on((3, 5, 4))
    for k, cp in ((-1, p1), (1, m1), (-3, p3), (3, m3)):
        cp.wait_recv()
        gc.append(send(h_piece(k), h_piece(k), partner))
    p4.wait_recv()
    m4.wait_recv()
    gc.append(send(h_piece(4), h_piece(4), partner))
    counts_copy.wait()
    map_copy.wait()
    for cp in gx + gc:
        cp.wait_recv()

    per = (NY * jw) // gpt

    def w_tile(r):
        return wbuf[r // per, pl.ds(lax.rem(r, per) * gpt, gpt)].reshape(tile, topics)

    def h_tile(q):
        return hbuf[pl.ds(q * gpt, gpt)].reshape(tile, topics)

    def ratio_step(i, carry):
        for u in range(4):
            s = i * 4 + u
            model = lax.dot_general(w_tile(rows_s[s]), h_tile(cols_s[s]), (((1,), (1,)), ((), ())),
                                    preferred_element_type=F32)
            ratio = counts[s].astype(F32) / model
            rat[s] = ratio.astype(BF16)
            rat_t[s] = ratio.T.astype(BF16)
        return carry

    lax.fori_loop(0, slots // 4, ratio_step, 0)

    wg = tr // NX
    zg = NZ // 4
    hg = tc // 4
    rx = {}
    for k in (2, 1, 3, 0):
        xx = at_x(k)
        lhs = jnp.concatenate([
            jnp.concatenate([rat[map_s[xx * wg + i, q]] for q in range(tc)], axis=1)
            for i in range(wg)], axis=0)
        out = jnp.dot(lhs, hbuf[...].reshape(tc * tile, topics), preferred_element_type=F32)
        out = out.reshape(NY * jw, SUB, topics)
        if k == 0:
            wfull[...] = out
        else:
            wp[k - 1] = encode(out)
            for j in FAR + (0,):
                at = pl.ds(at_y(j) * jw, jw)
                rx[j, k] = send(wp.at[k - 1, at], wx_in.at[k - 1, at], to_x(k))
    rc = {}
    for k in (2, 1, 3, 0):
        qq = lax.rem(z // zg + k, 4)
        lhs = jnp.concatenate([
            jnp.concatenate([rat_t[map_s[r, qq * hg + i]] for r in range(tr)], axis=1)
            for i in range(hg)], axis=0)
        out = jnp.dot(lhs, wbuf[...].reshape(tr * tile, topics), preferred_element_type=F32)
        out = out.reshape(hg * gpt, SUB, topics)
        at = pl.ds(qq * hg * gpt, hg * gpt)
        hfull[at] = out
        hp[at] = encode(out)
        zz = qq * zg
        rc[k] = [send(hp.at[pl.ds(((zz + i) * NC + 1 - c) * jh, jh)], hc_in.at[zz + i], partner)
                 for i in range(zg)]

    ones = jnp.ones((8, tile), BF16)
    sum_h = jnp.zeros((8, topics), F32)
    for q in range(tc):
        sum_h += jnp.dot(ones, h_tile(q), preferred_element_type=F32)
    cs_out[...] = sum_h
    cs_x = [send(cs_out, cs_x_in.at[k - 1], to_x(k)) for k in range(1, NX)]
    sum_w = jnp.zeros((8, topics), F32)
    for r in range(tr):
        sum_w += jnp.dot(ones, w_tile(r), preferred_element_type=F32)
    cd_out[...] = sum_w
    cd_c = send(cd_out, cd_c_in, partner)

    for k in (2, 1, 3, 0):
        for cp in rc[k]:
            cp.wait_recv()

    def both(k):
        zz = at_z(k)
        return hfull[pl.ds((zz * NC + c) * jh, jh)] + decode(hc_in[zz])

    hz_mid[0] = encode(both(4))
    q4p = send(hz_mid.at[0, pl.ds(0, hh)], h4_in.at[0], to_z(2))
    q4m = send(hz_mid.at[0, pl.ds(hh, hh)], h4_in.at[1], to_z(-2))
    hz_mid[1] = encode(both(3))
    q3p = send(hz_mid.at[1], h3_in.at[0], to_z(1))
    hz_mid[2] = encode(both(-3))
    q3m = send(hz_mid.at[2], h3_in.at[1], to_z(-1))
    hz_mid[3] = encode(both(1))
    q1p = send(hz_mid.at[3], hz_in.at[0], to_z(1))
    hz_mid[4] = encode(both(-1))
    q1m = send(hz_mid.at[4], hz_in.at[1], to_z(-1))

    ry = []

    def w_sum(ks):
        for j in ks:
            at = pl.ds(at_y(j) * jw, jw)
            for k in (1, 3, 2):
                rx[j, k].wait_recv()
            total = wfull[at]
            for k in range(NX - 1):
                total += decode(wx_in[k, at])
            if j == 0:
                return total
            wy_mid[j - 1] = encode(total)
            ry.append(send(wy_mid.at[j - 1], wy_in.at[j - 1], to_y(j)))

    w_sum((4, 3, 5))
    q3p.wait_recv()
    q4p.wait_recv()
    s2 = both(2) + decode(h3_in[0])
    hz_mid[5, pl.ds(0, hh)] = encode(s2[:hh] + decode(h4_in[0]))
    hz_mid[5, pl.ds(hh, hh)] = encode(s2[hh:])
    q2p = send(hz_mid.at[5], hz_in.at[2], to_z(2))
    q3m.wait_recv()
    q4m.wait_recv()
    s2 = both(-2) + decode(h3_in[1])
    hz_mid[6, pl.ds(0, hh)] = encode(s2[:hh])
    hz_mid[6, pl.ds(hh, hh)] = encode(s2[hh:] + decode(h4_in[1]))
    q2m = send(hz_mid.at[6], hz_in.at[3], to_z(-2))
    w_sum((2, 6, 1, 7))

    for cp in cs_x:
        cp.wait_recv()
    part = cs_out[...]
    for k in range(NX - 1):
        part += cs_x_in[k]
    cs_mid[...] = part
    cs_y = [send(cs_mid, cs_y_in.at[k - 1], to_y(k)) for k in FAR]
    cd_c.wait_recv()
    cd_mid[...] = cd_out[...] + cd_c_in[...]
    cd_z = [send(cd_mid, cd_z_in.at[k - 1], to_z(k)) for k in FAR]

    own_w = w_sum((0,))
    own_h = both(0)
    for cp in cd_z + [q1p, q1m, q2p, q2m]:
        cp.wait_recv()
    den = cd_mid[...]
    for k in range(NZ - 1):
        den += cd_z_in[k]
    for k in range(4):
        own_h += decode(hz_in[k])
    ho_ref[...] = (h_ref[...].astype(F32) * own_h / den[0:1].reshape(1, 1, topics)).astype(BF16)

    for cp in cs_y + ry:
        cp.wait_recv()
    den = cs_mid[...]
    for k in range(NY - 1):
        den += cs_y_in[k]
    for k in range(NY - 1):
        own_w += decode(wy_in[k])
    wo_ref[...] = (w_ref[...].astype(F32) * own_w / den[0:1].reshape(1, 1, topics)).astype(BF16)

    assert len(sent) == COPIES, len(sent)
    for cp in sent:
        cp.wait_send()


COPIES = (3 * 8 + 7) + (8 + 8) + 3 * 8 + 8 + 4 + 8 + 7 + 7 + 7


def body(w_factor, h_factor, tile_counts, tile_rows, tile_cols, tile_live):
    topics = w_factor.shape[1]
    slots, tile = tile_counts.shape[2], tile_counts.shape[3]
    tr = w_factor.shape[0] * NX * NY // tile
    tc = h_factor.shape[0] * NZ * NC // tile
    jw, jh = w_factor.shape[0] // SUB, h_factor.shape[0] // SUB

    vmem = pl.BlockSpec(memory_space=pltpu.VMEM)
    smem = pl.BlockSpec(memory_space=pltpu.SMEM)

    def V(*shape, dtype=BF16):
        return pltpu.VMEM(shape, dtype)

    def rows(*lead, dtype=BF16):
        return V(*lead, SUB, topics, dtype=dtype)

    def line(*lead):
        return V(*lead, 8, topics, dtype=F32)

    w_next, h_next = pl.pallas_call(
        functools.partial(kernel, tr, tc, slots, tile),
        out_shape=(jax.ShapeDtypeStruct((jw, SUB, topics), BF16),
                   jax.ShapeDtypeStruct((jh, SUB, topics), BF16)),
        in_specs=[smem, smem, smem, vmem, vmem, pl.BlockSpec(memory_space=pl.ANY)],
        out_specs=(vmem, vmem),
        scratch_shapes=[
            rows(NX, NY * jw), rows(NZ * NC * jh),
            V(slots, tile, tile), V(slots + 1, tile, tile), V(slots + 1, tile, tile),
            rows(NY * jw, dtype=F32), rows(NX - 1, NY * jw),
            rows(NZ * NC * jh, dtype=F32), rows(NZ * NC * jh),
            rows(NX - 1, NY * jw), rows(NY - 1, jw), rows(NY - 1, jw),
            rows(NZ, jh), rows(7, jh), rows(2, jh), rows(2, jh // 2), rows(4, jh),
            line(), line(NX - 1), line(), line(NY - 1),
            line(), line(), line(), line(NZ - 1),
            V(16, 128, dtype=jnp.int32), pltpu.SMEM((16, 128), jnp.int32),
            pltpu.SemaphoreType.DMA(()), pltpu.SemaphoreType.DMA(()),
            pltpu.SemaphoreType.DMA((COPIES,)), pltpu.SemaphoreType.DMA((COPIES,)),
        ],
        compiler_params=pltpu.CompilerParams(
            collective_id=0, has_side_effects=True, vmem_limit_bytes=56 << 20),
        name="update",
    )(tile_rows.reshape(slots), tile_cols.reshape(slots), tile_live,
      w_factor.reshape(jw, SUB, topics), h_factor.reshape(jh, SUB, topics),
      tile_counts.reshape(slots, tile, tile))
    return w_next.reshape(w_factor.shape), h_next.reshape(h_factor.shape)


def solution(mesh):
    in_specs = (
        P(("doc", "gram"), None),
        P(("gram", "doc"), None),
        P("doc", "gram", None, None, None),
        P("doc", "gram", None),
        P("doc", "gram", None),
        P("doc", "gram"),
    )
    out_specs = (P(("doc", "gram"), None), P(("gram", "doc"), None))
    return jax.shard_map(body, mesh=mesh, in_specs=in_specs, out_specs=out_specs, check_vma=False)
```

```python
import functools

import jax
import jax.numpy as jnp
from jax import lax
from jax.experimental import pallas as pl
from jax.experimental.pallas import tpu as pltpu
from jax.sharding import PartitionSpec as P

MESH = pl.DeviceIdType.MESH
NX, NY, NZ, NC = 4, 8, 8, 2
SUB = 16
F32 = jnp.float32
BF16 = jnp.bfloat16
NEAR = (1, 7, 2, 6, 3, 5, 4)
FAR = (4, 3, 5, 2, 6, 1, 7)


def encode(v):
    s = v * v
    return (s * s).astype(BF16)


def decode(code):
    return lax.rsqrt(lax.rsqrt(code.astype(F32)))


def kernel(tr, tc, slots, tile,
           live_s, rows_hbm, cols_hbm, w_ref, h_ref, counts_hbm, wo_ref, ho_ref,
           wbuf, hbuf, counts, rat, rat_t, wfull, wp, hfull, hp,
           wx_in, wy_mid, wy_in, hc_in, hz_mid, h3_in, h4_in, hz_in,
           cs_out, cs_x_in, cs_mid, cs_y_in, cd_out, cd_c_in, cd_mid, cd_z_in,
           rows_s, cols_s, map_v, map_s, loc_sem, ss, rs):
    doc = lax.axis_index("doc")
    gram = lax.axis_index("gram")
    z, c = doc // NC, lax.rem(doc, NC)
    x, y = gram // NY, lax.rem(gram, NY)
    jw = wbuf.shape[1] // NY
    jh = hbuf.shape[0] // (NZ * NC)
    hh = jh // 2
    gpt = tile // SUB
    topics = w_ref.shape[-1]
    sent = []

    def send(src, dst, to):
        i = len(sent)
        cp = pltpu.make_async_remote_copy(
            src_ref=src, dst_ref=dst, send_sem=ss.at[i], recv_sem=rs.at[i],
            device_id=to, device_id_type=MESH)
        cp.start()
        sent.append(cp)
        return cp

    def at_x(k):
        return lax.rem(x + NX + k, NX)

    def at_y(k):
        return lax.rem(y + NY + k, NY)

    def at_z(k):
        return lax.rem(z + NZ + k, NZ)

    def to_x(k):
        return doc, at_x(k) * NY + y

    def to_y(k):
        return doc, x * NY + at_y(k)

    def to_z(k):
        return at_z(k) * NC + c, gram

    partner = (z * NC + (1 - c), gram)

    barrier = pltpu.get_barrier_semaphore()
    peers = [to_y(k) for k in FAR] + [to_z(k) for k in FAR] + [to_x(k) for k in (2, 1, 3)] + [partner]
    for peer in peers:
        pl.semaphore_signal(barrier, inc=1, device_id=peer, device_id_type=MESH)
    local = [(rows_hbm, rows_s), (cols_hbm, cols_s),
             (w_ref, wbuf.at[x, pl.ds(y * jw, jw)]), (h_ref, hbuf.at[pl.ds(doc * jh, jh)]),
             (counts_hbm, counts)]
    local = [pltpu.make_async_copy(src, dst, loc_sem.at[i]) for i, (src, dst) in enumerate(local)]
    for cp in local:
        cp.start()
    pl.semaphore_wait(barrier, len(peers))

    def w_piece(k):
        return wbuf.at[x, pl.ds(at_y(k) * jw, jw)]

    def h_piece(k):
        return hbuf.at[pl.ds((at_z(k) * NC + c) * jh, jh)]

    def h_half(k, i):
        return hbuf.at[pl.ds((at_z(k) * NC + c) * jh + i * hh, hh)]

    gx = [send(w_ref, w_piece(0), to_x(k)) for k in (1, 3, 2)]
    gy = {k: send(w_ref, w_piece(0), to_y(k)) for k in NEAR}
    p2 = send(h_ref, h_piece(0), to_z(2))
    m2 = send(h_ref, h_piece(0), to_z(-2))
    p1 = send(h_ref, h_piece(0), to_z(1))
    m1 = send(h_ref, h_piece(0), to_z(-1))
    gc = [send(h_ref, h_piece(0), partner)]

    for cp in local[:2]:
        cp.wait()
    at_row = lax.broadcasted_iota(jnp.int32, map_v.shape, 0)
    at_col = lax.broadcasted_iota(jnp.int32, map_v.shape, 1)
    place = jnp.full(map_v.shape, slots, jnp.int32)
    for s in range(slots):
        row = jnp.where(s < live_s[0, 0], rows_s[s], -1)
        place = jnp.where((at_row == row) & (at_col == cols_s[s]), s, place)
    map_v[...] = place
    rat[slots] = jnp.zeros((tile, tile), BF16)
    rat_t[slots] = jnp.zeros((tile, tile), BF16)

    def w_on(ks):
        for k in ks:
            gy[k].wait_recv()
            gx.extend(send(w_piece(-k), w_piece(-k), to_x(j)) for j in (1, 3, 2))

    w_on((1, 7, 2, 6))
    map_copy = pltpu.make_async_copy(map_v, map_s, loc_sem.at[len(local)])
    map_copy.start()
    p2.wait_recv()
    p3 = send(h_piece(-2), h_piece(-2), to_z(1))
    p4 = send(h_half(-2, 0), h_half(-2, 0), to_z(2))
    m2.wait_recv()
    m3 = send(h_piece(2), h_piece(2), to_z(-1))
    m4 = send(h_half(2, 1), h_half(2, 1), to_z(-2))
    gc += [send(h_piece(-2), h_piece(-2), partner), send(h_piece(2), h_piece(2), partner)]
    w_on((3, 5, 4))
    for k, cp in ((-1, p1), (1, m1), (-3, p3), (3, m3)):
        cp.wait_recv()
        gc.append(send(h_piece(k), h_piece(k), partner))
    p4.wait_recv()
    m4.wait_recv()
    gc.append(send(h_piece(4), h_piece(4), partner))
    for cp in local[2:]:
        cp.wait()
    map_copy.wait()
    def column_sums(buf):
        return jnp.sum(buf[...].astype(F32).reshape(-1, 8, topics), axis=0)

    for cp in gc:
        cp.wait_recv()
    cs_out[...] = column_sums(hbuf)
    cs_x = [send(cs_out, cs_x_in.at[k - 1], to_x(k)) for k in range(1, NX)]
    for cp in gx:
        cp.wait_recv()
    cd_out[...] = column_sums(wbuf)
    cd_c = send(cd_out, cd_c_in, partner)

    per = (NY * jw) // gpt

    def w_tile(r):
        return wbuf[r // per, pl.ds(lax.rem(r, per) * gpt, gpt)].reshape(tile, topics)

    def h_tile(q):
        return hbuf[pl.ds(q * gpt, gpt)].reshape(tile, topics)

    def ratio_step(i, carry):
        for u in range(12):
            s = i * 12 + u
            model = lax.dot_general(w_tile(rows_s[s]), h_tile(cols_s[s]), (((1,), (1,)), ((), ())),
                                    preferred_element_type=F32)
            ratio = (counts[s].astype(F32) / model).astype(BF16)
            rat[s] = ratio
            rat_t[s] = ratio.T
        return carry

    lax.fori_loop(0, slots // 12, ratio_step, 0)

    wg = tr // NX
    zg = NZ // 4
    hg = tc // 4
    for cp in cs_x:
        cp.wait_recv()
    part = cs_out[...]
    for k in range(NX - 1):
        part += cs_x_in[k]
    cs_mid[...] = part
    cs_y = [send(cs_mid, cs_y_in.at[k - 1], to_y(k)) for k in FAR]
    cd_c.wait_recv()
    cd_mid[...] = cd_out[...] + cd_c_in[...]
    cd_z = [send(cd_mid, cd_z_in.at[k - 1], to_z(k)) for k in FAR]

    rx = {}
    for k in (2, 1, 3, 0):
        xx = at_x(k)
        lhs = jnp.concatenate([
            jnp.concatenate([rat[map_s[xx * wg + i, q]] for q in range(tc)], axis=1)
            for i in range(wg)], axis=0)
        out = jnp.dot(lhs, hbuf[...].reshape(tc * tile, topics), preferred_element_type=F32)
        out = out.reshape(NY * jw, SUB, topics)
        if k == 0:
            wfull[...] = out
        else:
            wp[k - 1] = encode(out)
        if k == 3:
            for j in FAR + (0,):
                at = pl.ds(at_y(j) * jw, jw)
                for i in (2, 1, 3):
                    rx[j, i] = send(wp.at[i - 1, at], wx_in.at[i - 1, at], to_x(i))
    rc = {}
    for k in (2, 1, 3, 0):
        qq = lax.rem(z // zg + k, 4)
        lhs = jnp.concatenate([
            jnp.concatenate([rat_t[map_s[r, qq * hg + i]] for r in range(tr)], axis=1)
            for i in range(hg)], axis=0)
        out = jnp.dot(lhs, wbuf[...].reshape(tr * tile, topics), preferred_element_type=F32)
        out = out.reshape(hg * gpt, SUB, topics)
        at = pl.ds(qq * hg * gpt, hg * gpt)
        hfull[at] = out
        hp[at] = encode(out)
        zz = qq * zg
        rc[k] = [send(hp.at[pl.ds(((zz + i) * NC + 1 - c) * jh, jh)], hc_in.at[zz + i], partner)
                 for i in range(zg)]

    left = []

    def drain(cps):
        for cp in cps:
            cp.wait_send()
        left.extend(cps)

    drain(gx + gc + list(gy.values()) + [p1, m1, p2, m2, p3, m3, p4, m4])

    for k in (2, 1, 3, 0):
        for cp in rc[k]:
            cp.wait_recv()

    def both(k):
        zz = at_z(k)
        return hfull[pl.ds((zz * NC + c) * jh, jh)] + decode(hc_in[zz])

    hz_mid[0] = encode(both(4))
    q4p = send(hz_mid.at[0, pl.ds(0, hh)], h4_in.at[0], to_z(2))
    q4m = send(hz_mid.at[0, pl.ds(hh, hh)], h4_in.at[1], to_z(-2))
    hz_mid[1] = encode(both(3))
    q3p = send(hz_mid.at[1], h3_in.at[0], to_z(1))
    hz_mid[2] = encode(both(-3))
    q3m = send(hz_mid.at[2], h3_in.at[1], to_z(-1))
    hz_mid[3] = encode(both(1))
    q1p = send(hz_mid.at[3], hz_in.at[0], to_z(1))
    hz_mid[4] = encode(both(-1))
    q1m = send(hz_mid.at[4], hz_in.at[1], to_z(-1))

    ry = []

    def w_sum(ks):
        for j in ks:
            at = pl.ds(at_y(j) * jw, jw)
            for k in (1, 3, 2):
                rx[j, k].wait_recv()
            total = wfull[at]
            for k in range(NX - 1):
                total += decode(wx_in[k, at])
            if j == 0:
                return total
            wy_mid[j - 1] = encode(total)
            ry.append(send(wy_mid.at[j - 1], wy_in.at[j - 1], to_y(j)))

    w_sum((4, 3, 5))
    q3p.wait_recv()
    q4p.wait_recv()
    s2 = both(2) + decode(h3_in[0])
    hz_mid[5, pl.ds(0, hh)] = encode(s2[:hh] + decode(h4_in[0]))
    hz_mid[5, pl.ds(hh, hh)] = encode(s2[hh:])
    q2p = send(hz_mid.at[5], hz_in.at[2], to_z(2))
    q3m.wait_recv()
    q4m.wait_recv()
    s2 = both(-2) + decode(h3_in[1])
    hz_mid[6, pl.ds(0, hh)] = encode(s2[:hh])
    hz_mid[6, pl.ds(hh, hh)] = encode(s2[hh:] + decode(h4_in[1]))
    q2m = send(hz_mid.at[6], hz_in.at[3], to_z(-2))
    w_sum((2, 6, 1, 7))

    drain(list(rx.values()) + sum(rc.values(), []) + cs_x + [cd_c, q4p, q4m, q3p, q3m])

    own_w = w_sum((0,))
    own_h = both(0)
    for cp in cd_z + [q1p, q1m, q2p, q2m]:
        cp.wait_recv()
    den = cd_mid[...]
    for k in range(NZ - 1):
        den += cd_z_in[k]
    for k in range(4):
        own_h += decode(hz_in[k])
    ho_ref[...] = (hbuf[pl.ds(doc * jh, jh)].astype(F32) * own_h / jnp.sum(den, axis=0).reshape(1, 1, topics)).astype(BF16)

    for cp in cs_y + ry:
        cp.wait_recv()
    den = cs_mid[...]
    for k in range(NY - 1):
        den += cs_y_in[k]
    for k in range(NY - 1):
        own_w += decode(wy_in[k])
    wo_ref[...] = (wbuf[x, pl.ds(y * jw, jw)].astype(F32) * own_w / jnp.sum(den, axis=0).reshape(1, 1, topics)).astype(BF16)

    assert len(sent) == COPIES, len(sent)
    for cp in sent:
        if not any(cp is done for done in left):
            cp.wait_send()


COPIES = (3 * 8 + 7) + (8 + 8) + 3 * 8 + 8 + 4 + 8 + 7 + 7 + 7


def body(w_factor, h_factor, tile_counts, tile_rows, tile_cols, tile_live):
    topics = w_factor.shape[1]
    slots, tile = tile_counts.shape[2], tile_counts.shape[3]
    tr = w_factor.shape[0] * NX * NY // tile
    tc = h_factor.shape[0] * NZ * NC // tile
    jw, jh = w_factor.shape[0] // SUB, h_factor.shape[0] // SUB

    vmem = pl.BlockSpec(memory_space=pltpu.VMEM)

    def V(*shape, dtype=BF16):
        return pltpu.VMEM(shape, dtype)

    def rows(*lead, dtype=BF16):
        return V(*lead, SUB, topics, dtype=dtype)

    def line(*lead):
        return V(*lead, 8, topics, dtype=F32)

    w_next, h_next = pl.pallas_call(
        functools.partial(kernel, tr, tc, slots, tile),
        out_shape=(jax.ShapeDtypeStruct((jw, SUB, topics), BF16),
                   jax.ShapeDtypeStruct((jh, SUB, topics), BF16)),
        in_specs=[pl.BlockSpec(memory_space=pltpu.SMEM)] + [pl.BlockSpec(memory_space=pltpu.HBM)] * 5,
        out_specs=(vmem, vmem),
        scratch_shapes=[
            rows(NX, NY * jw), rows(NZ * NC * jh),
            V(slots, tile, tile), V(slots + 1, tile, tile), V(slots + 1, tile, tile),
            rows(NY * jw, dtype=F32), rows(NX - 1, NY * jw),
            rows(NZ * NC * jh, dtype=F32), rows(NZ * NC * jh),
            rows(NX - 1, NY * jw), rows(NY - 1, jw), rows(NY - 1, jw),
            rows(NZ, jh), rows(7, jh), rows(2, jh), rows(2, jh // 2), rows(4, jh),
            line(), line(NX - 1), line(), line(NY - 1),
            line(), line(), line(), line(NZ - 1),
            pltpu.SMEM((slots,), jnp.int32), pltpu.SMEM((slots,), jnp.int32),
            V(16, 128, dtype=jnp.int32), pltpu.SMEM((16, 128), jnp.int32),
            pltpu.SemaphoreType.DMA((6,)),
            pltpu.SemaphoreType.DMA((COPIES,)), pltpu.SemaphoreType.DMA((COPIES,)),
        ],
        compiler_params=pltpu.CompilerParams(
            collective_id=0, has_side_effects=True, vmem_limit_bytes=24 << 20),
        name="update",
    )(tile_live, *(pltpu.with_memory_space_constraint(a, pltpu.HBM) for a in (
        tile_rows.reshape(slots), tile_cols.reshape(slots),
        w_factor.reshape(jw, SUB, topics), h_factor.reshape(jh, SUB, topics),
        tile_counts.reshape(slots, tile, tile))))
    return w_next.reshape(w_factor.shape), h_next.reshape(h_factor.shape)


def solution(mesh):
    in_specs = (
        P(("doc", "gram"), None),
        P(("gram", "doc"), None),
        P("doc", "gram", None, None, None),
        P("doc", "gram", None),
        P("doc", "gram", None),
        P("doc", "gram"),
    )
    out_specs = (P(("doc", "gram"), None), P(("gram", "doc"), None))
    return jax.shard_map(body, mesh=mesh, in_specs=in_specs, out_specs=out_specs, check_vma=False)
```

```python
import functools

import jax
import jax.numpy as jnp
from jax import lax
from jax.experimental import pallas as pl
from jax.experimental.pallas import tpu as pltpu
from jax.sharding import PartitionSpec as P

MESH = pl.DeviceIdType.MESH
NX, NY, NZ, NC = 4, 8, 8, 2
SUB = 16
F32 = jnp.float32
BF16 = jnp.bfloat16
NEAR = (1, 7, 2, 6, 3, 5, 4)
FAR = (4, 3, 5, 2, 6, 1, 7)


def encode(v):
    s = v * v
    return (s * s).astype(BF16)


def decode(code):
    return lax.rsqrt(lax.rsqrt(code.astype(F32)))


def kernel(tr, tc, slots, tile,
           live_s, rows_hbm, cols_hbm, w_ref, h_ref, counts_hbm, wo_ref, ho_ref,
           wbuf, hbuf, counts, rat, rat_t, wfull, wp, hfull, hp,
           wx_in, wy_mid, wy_in, hc_in, hz_mid, h3_in, h4_in, hz_in,
           cs_out, cs_x_in, cs_mid, cs_y_in, cd_out, cd_c_in, cd_mid, cd_z_in,
           rows_s, cols_s, map_v, map_s, loc_sem, ss, rs):
    doc = lax.axis_index("doc")
    gram = lax.axis_index("gram")
    z, c = doc // NC, lax.rem(doc, NC)
    x, y = gram // NY, lax.rem(gram, NY)
    jw = wbuf.shape[1] // NY
    jh = hbuf.shape[0] // (NZ * NC)
    hh = jh // 2
    gpt = tile // SUB
    topics = w_ref.shape[-1]
    sent = []

    def send(src, dst, to):
        i = len(sent)
        cp = pltpu.make_async_remote_copy(
            src_ref=src, dst_ref=dst, send_sem=ss.at[i], recv_sem=rs.at[i],
            device_id=to, device_id_type=MESH)
        cp.start()
        sent.append(cp)
        return cp

    def at_x(k):
        return lax.rem(x + NX + k, NX)

    def at_y(k):
        return lax.rem(y + NY + k, NY)

    def at_z(k):
        return lax.rem(z + NZ + k, NZ)

    def to_x(k):
        return doc, at_x(k) * NY + y

    def to_y(k):
        return doc, x * NY + at_y(k)

    def to_z(k):
        return at_z(k) * NC + c, gram

    partner = (z * NC + (1 - c), gram)

    barrier = pltpu.get_barrier_semaphore()
    peers = [to_y(k) for k in FAR] + [to_z(k) for k in FAR] + [to_x(k) for k in (2, 1, 3)] + [partner]
    for peer in peers:
        pl.semaphore_signal(barrier, inc=1, device_id=peer, device_id_type=MESH)
    local = [(rows_hbm, rows_s), (cols_hbm, cols_s),
             (w_ref, wbuf.at[x, pl.ds(y * jw, jw)]), (h_ref, hbuf.at[pl.ds(doc * jh, jh)]),
             (counts_hbm, counts)]
    local = [pltpu.make_async_copy(src, dst, loc_sem.at[i]) for i, (src, dst) in enumerate(local)]
    for cp in local:
        cp.start()
    pl.semaphore_wait(barrier, len(peers))

    def w_piece(k):
        return wbuf.at[x, pl.ds(at_y(k) * jw, jw)]

    def h_piece(k):
        return hbuf.at[pl.ds((at_z(k) * NC + c) * jh, jh)]

    def h_half(k, i):
        return hbuf.at[pl.ds((at_z(k) * NC + c) * jh + i * hh, hh)]

    gx = [send(w_ref, w_piece(0), to_x(k)) for k in (1, 3, 2)]
    gy = {k: send(w_ref, w_piece(0), to_y(k)) for k in NEAR}
    p2 = send(h_ref, h_piece(0), to_z(2))
    m2 = send(h_ref, h_piece(0), to_z(-2))
    p1 = send(h_ref, h_piece(0), to_z(1))
    m1 = send(h_ref, h_piece(0), to_z(-1))
    gc = [send(h_ref, h_piece(0), partner)]

    for cp in local[:2]:
        cp.wait()
    at_row = lax.broadcasted_iota(jnp.int32, map_v.shape, 0)
    at_col = lax.broadcasted_iota(jnp.int32, map_v.shape, 1)
    place = jnp.full(map_v.shape, slots, jnp.int32)
    for s in range(slots):
        row = jnp.where(s < live_s[0, 0], rows_s[s], -1)
        place = jnp.where((at_row == row) & (at_col == cols_s[s]), s, place)
    map_v[...] = place
    rat[slots] = jnp.zeros((tile, tile), BF16)
    rat_t[slots] = jnp.zeros((tile, tile), BF16)

    def w_on(ks):
        for k in ks:
            gy[k].wait_recv()
            gx.extend(send(w_piece(-k), w_piece(-k), to_x(j)) for j in (1, 3, 2))

    w_on((1, 7))
    map_copy = pltpu.make_async_copy(map_v, map_s, loc_sem.at[len(local)])
    map_copy.start()
    p2.wait_recv()
    p3 = send(h_piece(-2), h_piece(-2), to_z(1))
    p4 = send(h_half(-2, 0), h_half(-2, 0), to_z(2))
    m2.wait_recv()
    m3 = send(h_piece(2), h_piece(2), to_z(-1))
    m4 = send(h_half(2, 1), h_half(2, 1), to_z(-2))
    gc += [send(h_piece(-2), h_piece(-2), partner), send(h_piece(2), h_piece(2), partner)]
    w_on((2, 6, 3, 5, 4))
    for k, cp in ((-1, p1), (1, m1), (-3, p3), (3, m3)):
        cp.wait_recv()
        gc.append(send(h_piece(k), h_piece(k), partner))
    p4.wait_recv()
    m4.wait_recv()
    gc.append(send(h_piece(4), h_piece(4), partner))
    for cp in local[2:]:
        cp.wait()
    map_copy.wait()
    def column_sums(buf):
        return jnp.sum(buf[...].astype(F32).reshape(-1, 8, topics), axis=0)

    for cp in gc:
        cp.wait_recv()
    cs_out[...] = column_sums(hbuf)
    cs_x = [send(cs_out, cs_x_in.at[k - 1], to_x(k)) for k in range(1, NX)]
    for cp in gx:
        cp.wait_recv()
    cd_out[...] = column_sums(wbuf)
    cd_c = send(cd_out, cd_c_in, partner)

    per = (NY * jw) // gpt

    def w_tile(r):
        return wbuf[r // per, pl.ds(lax.rem(r, per) * gpt, gpt)].reshape(tile, topics)

    def h_tile(q):
        return hbuf[pl.ds(q * gpt, gpt)].reshape(tile, topics)

    def ratio_step(i, carry):
        for u in range(12):
            s = i * 12 + u
            model = lax.dot_general(w_tile(rows_s[s]), h_tile(cols_s[s]), (((1,), (1,)), ((), ())),
                                    preferred_element_type=F32)
            ratio = (counts[s].astype(F32) / model).astype(BF16)
            rat[s] = ratio
            rat_t[s] = ratio.T
        return carry

    lax.fori_loop(0, slots // 12, ratio_step, 0)

    wg = tr // NX
    zg = NZ // 4
    hg = tc // 4
    for cp in cs_x:
        cp.wait_recv()
    part = cs_out[...]
    for k in range(NX - 1):
        part += cs_x_in[k]
    cs_mid[...] = part
    cs_y = [send(cs_mid, cs_y_in.at[k - 1], to_y(k)) for k in FAR]
    cd_c.wait_recv()
    cd_mid[...] = cd_out[...] + cd_c_in[...]
    cd_z = [send(cd_mid, cd_z_in.at[k - 1], to_z(k)) for k in FAR]

    rx = {}
    for k in (2, 1, 3, 0):
        xx = at_x(k)
        lhs = jnp.concatenate([
            jnp.concatenate([rat[map_s[xx * wg + i, q]] for q in range(tc)], axis=1)
            for i in range(wg)], axis=0)
        out = jnp.dot(lhs, hbuf[...].reshape(tc * tile, topics), preferred_element_type=F32)
        out = out.reshape(NY * jw, SUB, topics)
        if k == 0:
            wfull[...] = out
        else:
            wp[k - 1] = encode(out)
        if k == 3:
            for j in FAR + (0,):
                at = pl.ds(at_y(j) * jw, jw)
                for i in (2, 1, 3):
                    rx[j, i] = send(wp.at[i - 1, at], wx_in.at[i - 1, at], to_x(i))
    rc = {}
    for k in (2, 1, 3, 0):
        qq = lax.rem(z // zg + k, 4)
        lhs = jnp.concatenate([
            jnp.concatenate([rat_t[map_s[r, qq * hg + i]] for r in range(tr)], axis=1)
            for i in range(hg)], axis=0)
        out = jnp.dot(lhs, wbuf[...].reshape(tr * tile, topics), preferred_element_type=F32)
        out = out.reshape(hg * gpt, SUB, topics)
        at = pl.ds(qq * hg * gpt, hg * gpt)
        hfull[at] = out
        hp[at] = encode(out)
        zz = qq * zg
        rc[k] = [send(hp.at[pl.ds(((zz + i) * NC + 1 - c) * jh, jh)], hc_in.at[zz + i], partner)
                 for i in range(zg)]

    left = []

    def drain(cps):
        for cp in cps:
            cp.wait_send()
        left.extend(cps)

    drain(gx + gc + list(gy.values()) + [p1, m1, p2, m2, p3, m3, p4, m4])

    for k in (2, 1, 3, 0):
        for cp in rc[k]:
            cp.wait_recv()

    def both(k):
        zz = at_z(k)
        return hfull[pl.ds((zz * NC + c) * jh, jh)] + decode(hc_in[zz])

    hz_mid[0] = encode(both(4))
    q4p = send(hz_mid.at[0, pl.ds(0, hh)], h4_in.at[0], to_z(2))
    q4m = send(hz_mid.at[0, pl.ds(hh, hh)], h4_in.at[1], to_z(-2))
    hz_mid[1] = encode(both(3))
    q3p = send(hz_mid.at[1], h3_in.at[0], to_z(1))
    hz_mid[2] = encode(both(-3))
    q3m = send(hz_mid.at[2], h3_in.at[1], to_z(-1))
    hz_mid[3] = encode(both(1))
    q1p = send(hz_mid.at[3], hz_in.at[0], to_z(1))
    hz_mid[4] = encode(both(-1))
    q1m = send(hz_mid.at[4], hz_in.at[1], to_z(-1))

    ry = []

    def w_sum(ks):
        for j in ks:
            at = pl.ds(at_y(j) * jw, jw)
            for k in (1, 3, 2):
                rx[j, k].wait_recv()
            total = wfull[at]
            for k in range(NX - 1):
                total += decode(wx_in[k, at])
            if j == 0:
                return total
            wy_mid[j - 1] = encode(total)
            ry.append(send(wy_mid.at[j - 1], wy_in.at[j - 1], to_y(j)))

    w_sum((4, 3, 5))
    q3p.wait_recv()
    q4p.wait_recv()
    s2 = both(2) + decode(h3_in[0])
    hz_mid[5, pl.ds(0, hh)] = encode(s2[:hh] + decode(h4_in[0]))
    hz_mid[5, pl.ds(hh, hh)] = encode(s2[hh:])
    q2p = send(hz_mid.at[5], hz_in.at[2], to_z(2))
    q3m.wait_recv()
    q4m.wait_recv()
    s2 = both(-2) + decode(h3_in[1])
    hz_mid[6, pl.ds(0, hh)] = encode(s2[:hh])
    hz_mid[6, pl.ds(hh, hh)] = encode(s2[hh:] + decode(h4_in[1]))
    q2m = send(hz_mid.at[6], hz_in.at[3], to_z(-2))
    w_sum((2, 6, 1, 7))

    drain(list(rx.values()) + sum(rc.values(), []) + cs_x + [cd_c, q4p, q4m, q3p, q3m])

    own_w = w_sum((0,))
    own_h = both(0)
    for cp in cd_z + [q1p, q1m, q2p, q2m]:
        cp.wait_recv()
    den = cd_mid[...]
    for k in range(NZ - 1):
        den += cd_z_in[k]
    for k in range(4):
        own_h += decode(hz_in[k])
    ho_ref[...] = (hbuf[pl.ds(doc * jh, jh)].astype(F32) * own_h / jnp.sum(den, axis=0).reshape(1, 1, topics)).astype(BF16)

    for cp in cs_y + ry:
        cp.wait_recv()
    den = cs_mid[...]
    for k in range(NY - 1):
        den += cs_y_in[k]
    for k in range(NY - 1):
        own_w += decode(wy_in[k])
    wo_ref[...] = (wbuf[x, pl.ds(y * jw, jw)].astype(F32) * own_w / jnp.sum(den, axis=0).reshape(1, 1, topics)).astype(BF16)

    assert len(sent) == COPIES, len(sent)
    for cp in sent:
        if not any(cp is done for done in left):
            cp.wait_send()


def place(w_ref, h_ref, wo_ref, ho_ref, sem):
    copies = [pltpu.make_async_copy(w_ref, wo_ref, sem.at[0]), pltpu.make_async_copy(h_ref, ho_ref, sem.at[1])]
    for cp in copies:
        cp.start()
    for cp in copies:
        cp.wait()


COPIES = (3 * 8 + 7) + (8 + 8) + 3 * 8 + 8 + 4 + 8 + 7 + 7 + 7


def body(w_factor, h_factor, tile_counts, tile_rows, tile_cols, tile_live):
    topics = w_factor.shape[1]
    slots, tile = tile_counts.shape[2], tile_counts.shape[3]
    tr = w_factor.shape[0] * NX * NY // tile
    tc = h_factor.shape[0] * NZ * NC // tile
    jw, jh = w_factor.shape[0] // SUB, h_factor.shape[0] // SUB

    vmem = pl.BlockSpec(memory_space=pltpu.VMEM)

    def V(*shape, dtype=BF16):
        return pltpu.VMEM(shape, dtype)

    def rows(*lead, dtype=BF16):
        return V(*lead, SUB, topics, dtype=dtype)

    def line(*lead):
        return V(*lead, 8, topics, dtype=F32)

    w_next, h_next = pl.pallas_call(
        functools.partial(kernel, tr, tc, slots, tile),
        out_shape=(jax.ShapeDtypeStruct((jw, SUB, topics), BF16),
                   jax.ShapeDtypeStruct((jh, SUB, topics), BF16)),
        in_specs=[pl.BlockSpec(memory_space=pltpu.SMEM)] + [pl.BlockSpec(memory_space=pltpu.HBM)] * 5,
        out_specs=(vmem, vmem),
        scratch_shapes=[
            rows(NX, NY * jw), rows(NZ * NC * jh),
            V(slots, tile, tile), V(slots + 1, tile, tile), V(slots + 1, tile, tile),
            rows(NY * jw, dtype=F32), rows(NX - 1, NY * jw),
            rows(NZ * NC * jh, dtype=F32), rows(NZ * NC * jh),
            rows(NX - 1, NY * jw), rows(NY - 1, jw), rows(NY - 1, jw),
            rows(NZ, jh), rows(7, jh), rows(2, jh), rows(2, jh // 2), rows(4, jh),
            line(), line(NX - 1), line(), line(NY - 1),
            line(), line(), line(), line(NZ - 1),
            pltpu.SMEM((slots,), jnp.int32), pltpu.SMEM((slots,), jnp.int32),
            V(16, 128, dtype=jnp.int32), pltpu.SMEM((16, 128), jnp.int32),
            pltpu.SemaphoreType.DMA((6,)),
            pltpu.SemaphoreType.DMA((COPIES,)), pltpu.SemaphoreType.DMA((COPIES,)),
        ],
        compiler_params=pltpu.CompilerParams(
            collective_id=0, has_side_effects=True, vmem_limit_bytes=24 << 20),
        name="update",
    )(tile_live, *(pltpu.with_memory_space_constraint(a, pltpu.HBM) for a in (
        tile_rows.reshape(slots), tile_cols.reshape(slots),
        w_factor.reshape(jw, SUB, topics), h_factor.reshape(jh, SUB, topics),
        tile_counts.reshape(slots, tile, tile))))
    hbm = pl.BlockSpec(memory_space=pl.ANY)
    w_next, h_next = pl.pallas_call(
        place,
        out_shape=(jax.ShapeDtypeStruct((jw, SUB, topics), BF16),
                   jax.ShapeDtypeStruct((jh, SUB, topics), BF16)),
        in_specs=[hbm, hbm],
        out_specs=(pl.BlockSpec(memory_space=pltpu.HBM), pl.BlockSpec(memory_space=pltpu.HBM)),
        scratch_shapes=[pltpu.SemaphoreType.DMA((2,))],
        compiler_params=pltpu.CompilerParams(vmem_limit_bytes=1 << 20),
        name="place",
    )(w_next, h_next)
    return w_next.reshape(w_factor.shape), h_next.reshape(h_factor.shape)


def solution(mesh):
    in_specs = (
        P(("doc", "gram"), None),
        P(("gram", "doc"), None),
        P("doc", "gram", None, None, None),
        P("doc", "gram", None),
        P("doc", "gram", None),
        P("doc", "gram"),
    )
    out_specs = (P(("doc", "gram"), None), P(("gram", "doc"), None))
    return jax.shard_map(body, mesh=mesh, in_specs=in_specs, out_specs=out_specs, check_vma=False)
```

```python
import functools

import jax
import jax.numpy as jnp
from jax import lax
from jax.experimental import pallas as pl
from jax.experimental.pallas import tpu as pltpu
from jax.sharding import PartitionSpec as P

MESH = pl.DeviceIdType.MESH
NX, NY, NZ, NC = 4, 8, 8, 2
SUB = 16
F32 = jnp.float32
BF16 = jnp.bfloat16
NEAR = (1, 7, 2, 6, 3, 5, 4)
FAR = (4, 3, 5, 2, 6, 1, 7)


def encode(v):
    s = v * v
    return (s * s).astype(BF16)


def decode(code):
    return lax.rsqrt(lax.rsqrt(code.astype(F32)))


def kernel(tr, tc, slots, tile,
           live_s, rows_hbm, cols_hbm, w_ref, h_ref, counts_hbm, wo_ref, ho_ref,
           wbuf, hbuf, counts, rat, rat_t, wfull, wp, hfull, hp,
           wx_in, wy_mid, wy_in, hc_in, hz_mid, h3_in, h4_in, hz_in,
           cs_out, cs_x_in, cs_mid, cs_y_in, cd_out, cd_c_in, cd_mid, cd_z_in,
           rows_s, cols_s, map_v, map_s, loc_sem, ss, rs):
    doc = lax.axis_index("doc")
    gram = lax.axis_index("gram")
    z, c = doc // NC, lax.rem(doc, NC)
    x, y = gram // NY, lax.rem(gram, NY)
    jw = wbuf.shape[1] // NY
    jh = hbuf.shape[0] // (NZ * NC)
    hh = jh // 2
    gpt = tile // SUB
    topics = w_ref.shape[-1]
    sent = []

    def send(src, dst, to):
        i = len(sent)
        cp = pltpu.make_async_remote_copy(
            src_ref=src, dst_ref=dst, send_sem=ss.at[i], recv_sem=rs.at[i],
            device_id=to, device_id_type=MESH)
        cp.start()
        sent.append(cp)
        return cp

    def at_x(k):
        return lax.rem(x + NX + k, NX)

    def at_y(k):
        return lax.rem(y + NY + k, NY)

    def at_z(k):
        return lax.rem(z + NZ + k, NZ)

    def to_x(k):
        return doc, at_x(k) * NY + y

    def to_y(k):
        return doc, x * NY + at_y(k)

    def to_z(k):
        return at_z(k) * NC + c, gram

    partner = (z * NC + (1 - c), gram)

    barrier = pltpu.get_barrier_semaphore()
    peers = [to_y(k) for k in FAR] + [to_z(k) for k in FAR] + [to_x(k) for k in (2, 1, 3)] + [partner]
    for peer in peers:
        pl.semaphore_signal(barrier, inc=1, device_id=peer, device_id_type=MESH)
    local = [(rows_hbm, rows_s), (cols_hbm, cols_s),
             (w_ref, wbuf.at[x, pl.ds(y * jw, jw)]), (h_ref, hbuf.at[pl.ds(doc * jh, jh)]),
             (counts_hbm, counts)]
    local = [pltpu.make_async_copy(src, dst, loc_sem.at[i]) for i, (src, dst) in enumerate(local)]
    for cp in local:
        cp.start()
    pl.semaphore_wait(barrier, len(peers))

    def w_piece(k):
        return wbuf.at[x, pl.ds(at_y(k) * jw, jw)]

    def h_piece(k):
        return hbuf.at[pl.ds((at_z(k) * NC + c) * jh, jh)]

    def h_half(k, i):
        return hbuf.at[pl.ds((at_z(k) * NC + c) * jh + i * hh, hh)]

    gx = [send(w_ref, w_piece(0), to_x(k)) for k in (1, 3, 2)]
    gy = {k: send(w_ref, w_piece(0), to_y(k)) for k in NEAR}
    p2 = send(h_ref, h_piece(0), to_z(2))
    m2 = send(h_ref, h_piece(0), to_z(-2))
    p1 = send(h_ref, h_piece(0), to_z(1))
    m1 = send(h_ref, h_piece(0), to_z(-1))
    gc = [send(h_ref, h_piece(0), partner)]

    for cp in local[:2]:
        cp.wait()
    at_row = lax.broadcasted_iota(jnp.int32, map_v.shape, 0)
    at_col = lax.broadcasted_iota(jnp.int32, map_v.shape, 1)
    place = jnp.full(map_v.shape, slots, jnp.int32)
    for s in range(slots):
        row = jnp.where(s < live_s[0, 0], rows_s[s], -1)
        place = jnp.where((at_row == row) & (at_col == cols_s[s]), s, place)
    map_v[...] = place
    rat[slots] = jnp.zeros((tile, tile), BF16)
    rat_t[slots] = jnp.zeros((tile, tile), BF16)

    def w_on(ks):
        for k in ks:
            gy[k].wait_recv()
            gx.extend(send(w_piece(-k), w_piece(-k), to_x(j)) for j in (1, 3, 2))

    w_on((1, 7))
    map_copy = pltpu.make_async_copy(map_v, map_s, loc_sem.at[len(local)])
    map_copy.start()
    p2.wait_recv()
    p3 = send(h_piece(-2), h_piece(-2), to_z(1))
    p4 = send(h_half(-2, 0), h_half(-2, 0), to_z(2))
    m2.wait_recv()
    m3 = send(h_piece(2), h_piece(2), to_z(-1))
    m4 = send(h_half(2, 1), h_half(2, 1), to_z(-2))
    gc += [send(h_piece(-2), h_piece(-2), partner), send(h_piece(2), h_piece(2), partner)]
    w_on((2, 6))
    for k, cp in ((-1, p1), (1, m1)):
        cp.wait_recv()
        gc.append(send(h_piece(k), h_piece(k), partner))
    w_on((3, 5))
    for k, cp in ((-3, p3), (3, m3)):
        cp.wait_recv()
        gc.append(send(h_piece(k), h_piece(k), partner))
    w_on((4,))
    p4.wait_recv()
    m4.wait_recv()
    gc.append(send(h_piece(4), h_piece(4), partner))
    for cp in local[2:]:
        cp.wait()
    map_copy.wait()
    def column_sums(buf):
        return jnp.sum(buf[...].astype(F32).reshape(-1, 8, topics), axis=0)

    for cp in gc:
        cp.wait_recv()
    cs_out[...] = column_sums(hbuf)
    cs_x = [send(cs_out, cs_x_in.at[k - 1], to_x(k)) for k in range(1, NX)]
    for cp in gx:
        cp.wait_recv()
    cd_out[...] = column_sums(wbuf)
    cd_c = send(cd_out, cd_c_in, partner)

    per = (NY * jw) // gpt

    def w_tile(r):
        return wbuf[r // per, pl.ds(lax.rem(r, per) * gpt, gpt)].reshape(tile, topics)

    def h_tile(q):
        return hbuf[pl.ds(q * gpt, gpt)].reshape(tile, topics)

    def ratio_step(i, carry):
        for u in range(12):
            s = i * 12 + u
            model = lax.dot_general(w_tile(rows_s[s]), h_tile(cols_s[s]), (((1,), (1,)), ((), ())),
                                    preferred_element_type=F32)
            ratio = (counts[s].astype(F32) / model).astype(BF16)
            rat[s] = ratio
            rat_t[s] = ratio.T
        return carry

    lax.fori_loop(0, slots // 12, ratio_step, 0)

    wg = tr // NX
    zg = NZ // 4
    hg = tc // 4
    for cp in cs_x:
        cp.wait_recv()
    part = cs_out[...]
    for k in range(NX - 1):
        part += cs_x_in[k]
    cs_mid[...] = part
    cs_y = [send(cs_mid, cs_y_in.at[k - 1], to_y(k)) for k in FAR]
    cd_c.wait_recv()
    cd_mid[...] = cd_out[...] + cd_c_in[...]
    cd_z = [send(cd_mid, cd_z_in.at[k - 1], to_z(k)) for k in FAR]

    rx = {}
    for k in (2, 1, 3, 0):
        xx = at_x(k)
        lhs = jnp.concatenate([
            jnp.concatenate([rat[map_s[xx * wg + i, q]] for q in range(tc)], axis=1)
            for i in range(wg)], axis=0)
        out = jnp.dot(lhs, hbuf[...].reshape(tc * tile, topics), preferred_element_type=F32)
        out = out.reshape(NY * jw, SUB, topics)
        if k == 0:
            wfull[...] = out
        else:
            wp[k - 1] = encode(out)
        if k == 3:
            for j in FAR + (0,):
                at = pl.ds(at_y(j) * jw, jw)
                for i in (2, 1, 3):
                    rx[j, i] = send(wp.at[i - 1, at], wx_in.at[i - 1, at], to_x(i))
    rc = {}
    for k in (2, 1, 3, 0):
        qq = lax.rem(z // zg + k, 4)
        lhs = jnp.concatenate([
            jnp.concatenate([rat_t[map_s[r, qq * hg + i]] for r in range(tr)], axis=1)
            for i in range(hg)], axis=0)
        out = jnp.dot(lhs, wbuf[...].reshape(tr * tile, topics), preferred_element_type=F32)
        out = out.reshape(hg * gpt, SUB, topics)
        at = pl.ds(qq * hg * gpt, hg * gpt)
        hfull[at] = out
        hp[at] = encode(out)
        zz = qq * zg
        rc[k] = [send(hp.at[pl.ds(((zz + i) * NC + 1 - c) * jh, jh)], hc_in.at[zz + i], partner)
                 for i in range(zg)]

    left = []

    def drain(cps):
        for cp in cps:
            cp.wait_send()
        left.extend(cps)

    drain(gx + gc + list(gy.values()) + [p1, m1, p2, m2, p3, m3, p4, m4])

    for k in (2, 1, 3, 0):
        for cp in rc[k]:
            cp.wait_recv()

    def both(k):
        zz = at_z(k)
        return hfull[pl.ds((zz * NC + c) * jh, jh)] + decode(hc_in[zz])

    hz_mid[0] = encode(both(4))
    q4p = send(hz_mid.at[0, pl.ds(0, hh)], h4_in.at[0], to_z(2))
    q4m = send(hz_mid.at[0, pl.ds(hh, hh)], h4_in.at[1], to_z(-2))
    hz_mid[1] = encode(both(3))
    q3p = send(hz_mid.at[1], h3_in.at[0], to_z(1))
    hz_mid[2] = encode(both(-3))
    q3m = send(hz_mid.at[2], h3_in.at[1], to_z(-1))
    hz_mid[3] = encode(both(1))
    q1p = send(hz_mid.at[3], hz_in.at[0], to_z(1))
    hz_mid[4] = encode(both(-1))
    q1m = send(hz_mid.at[4], hz_in.at[1], to_z(-1))

    ry = []

    def w_sum(ks):
        for j in ks:
            at = pl.ds(at_y(j) * jw, jw)
            for k in (1, 3, 2):
                rx[j, k].wait_recv()
            total = wfull[at]
            for k in range(NX - 1):
                total += decode(wx_in[k, at])
            if j == 0:
                return total
            wy_mid[j - 1] = encode(total)
            ry.append(send(wy_mid.at[j - 1], wy_in.at[j - 1], to_y(j)))

    w_sum((4, 3, 5))
    q3p.wait_recv()
    q4p.wait_recv()
    s2 = both(2) + decode(h3_in[0])
    hz_mid[5, pl.ds(0, hh)] = encode(s2[:hh] + decode(h4_in[0]))
    hz_mid[5, pl.ds(hh, hh)] = encode(s2[hh:])
    q2p = send(hz_mid.at[5], hz_in.at[2], to_z(2))
    q3m.wait_recv()
    q4m.wait_recv()
    s2 = both(-2) + decode(h3_in[1])
    hz_mid[6, pl.ds(0, hh)] = encode(s2[:hh])
    hz_mid[6, pl.ds(hh, hh)] = encode(s2[hh:] + decode(h4_in[1]))
    q2m = send(hz_mid.at[6], hz_in.at[3], to_z(-2))
    w_sum((2, 6, 1, 7))

    drain(list(rx.values()) + sum(rc.values(), []) + cs_x + [cd_c, q4p, q4m, q3p, q3m])

    own_w = w_sum((0,))
    own_h = both(0)
    for cp in cd_z + [q1p, q1m, q2p, q2m]:
        cp.wait_recv()
    den = cd_mid[...]
    for k in range(NZ - 1):
        den += cd_z_in[k]
    for k in range(4):
        own_h += decode(hz_in[k])
    ho_ref[...] = (hbuf[pl.ds(doc * jh, jh)].astype(F32) * own_h / jnp.sum(den, axis=0).reshape(1, 1, topics)).astype(BF16)

    for cp in cs_y + ry:
        cp.wait_recv()
    den = cs_mid[...]
    for k in range(NY - 1):
        den += cs_y_in[k]
    for k in range(NY - 1):
        own_w += decode(wy_in[k])
    wo_ref[...] = (wbuf[x, pl.ds(y * jw, jw)].astype(F32) * own_w / jnp.sum(den, axis=0).reshape(1, 1, topics)).astype(BF16)

    assert len(sent) == COPIES, len(sent)
    for cp in sent:
        if not any(cp is done for done in left):
            cp.wait_send()


def place(w_ref, h_ref, wo_ref, ho_ref, sem):
    copies = [pltpu.make_async_copy(w_ref, wo_ref, sem.at[0]), pltpu.make_async_copy(h_ref, ho_ref, sem.at[1])]
    for cp in copies:
        cp.start()
    for cp in copies:
        cp.wait()


COPIES = (3 * 8 + 7) + (8 + 8) + 3 * 8 + 8 + 4 + 8 + 7 + 7 + 7


def body(w_factor, h_factor, tile_counts, tile_rows, tile_cols, tile_live):
    topics = w_factor.shape[1]
    slots, tile = tile_counts.shape[2], tile_counts.shape[3]
    tr = w_factor.shape[0] * NX * NY // tile
    tc = h_factor.shape[0] * NZ * NC // tile
    jw, jh = w_factor.shape[0] // SUB, h_factor.shape[0] // SUB

    vmem = pl.BlockSpec(memory_space=pltpu.VMEM)

    def V(*shape, dtype=BF16):
        return pltpu.VMEM(shape, dtype)

    def rows(*lead, dtype=BF16):
        return V(*lead, SUB, topics, dtype=dtype)

    def line(*lead):
        return V(*lead, 8, topics, dtype=F32)

    w_next, h_next = pl.pallas_call(
        functools.partial(kernel, tr, tc, slots, tile),
        out_shape=(jax.ShapeDtypeStruct((jw, SUB, topics), BF16),
                   jax.ShapeDtypeStruct((jh, SUB, topics), BF16)),
        in_specs=[pl.BlockSpec(memory_space=pltpu.SMEM)] + [pl.BlockSpec(memory_space=pltpu.HBM)] * 5,
        out_specs=(vmem, vmem),
        scratch_shapes=[
            rows(NX, NY * jw), rows(NZ * NC * jh),
            V(slots, tile, tile), V(slots + 1, tile, tile), V(slots + 1, tile, tile),
            rows(NY * jw, dtype=F32), rows(NX - 1, NY * jw),
            rows(NZ * NC * jh, dtype=F32), rows(NZ * NC * jh),
            rows(NX - 1, NY * jw), rows(NY - 1, jw), rows(NY - 1, jw),
            rows(NZ, jh), rows(7, jh), rows(2, jh), rows(2, jh // 2), rows(4, jh),
            line(), line(NX - 1), line(), line(NY - 1),
            line(), line(), line(), line(NZ - 1),
            pltpu.SMEM((slots,), jnp.int32), pltpu.SMEM((slots,), jnp.int32),
            V(16, 128, dtype=jnp.int32), pltpu.SMEM((16, 128), jnp.int32),
            pltpu.SemaphoreType.DMA((6,)),
            pltpu.SemaphoreType.DMA((COPIES,)), pltpu.SemaphoreType.DMA((COPIES,)),
        ],
        compiler_params=pltpu.CompilerParams(
            collective_id=0, has_side_effects=True, vmem_limit_bytes=24 << 20),
        name="update",
    )(tile_live, *(pltpu.with_memory_space_constraint(a, pltpu.HBM) for a in (
        tile_rows.reshape(slots), tile_cols.reshape(slots),
        w_factor.reshape(jw, SUB, topics), h_factor.reshape(jh, SUB, topics),
        tile_counts.reshape(slots, tile, tile))))
    hbm = pl.BlockSpec(memory_space=pl.ANY)
    w_next, h_next = pl.pallas_call(
        place,
        out_shape=(jax.ShapeDtypeStruct((jw, SUB, topics), BF16),
                   jax.ShapeDtypeStruct((jh, SUB, topics), BF16)),
        in_specs=[hbm, hbm],
        out_specs=(pl.BlockSpec(memory_space=pltpu.HBM), pl.BlockSpec(memory_space=pltpu.HBM)),
        scratch_shapes=[pltpu.SemaphoreType.DMA((2,))],
        compiler_params=pltpu.CompilerParams(vmem_limit_bytes=1 << 20),
        name="place",
    )(w_next, h_next)
    return w_next.reshape(w_factor.shape), h_next.reshape(h_factor.shape)


def solution(mesh):
    in_specs = (
        P(("doc", "gram"), None),
        P(("gram", "doc"), None),
        P("doc", "gram", None, None, None),
        P("doc", "gram", None),
        P("doc", "gram", None),
        P("doc", "gram"),
    )
    out_specs = (P(("doc", "gram"), None), P(("gram", "doc"), None))
    return jax.shard_map(body, mesh=mesh, in_specs=in_specs, out_specs=out_specs, check_vma=False)
```
